32 devices in a mesh: row: 4 (over z), col: 8 (over y, x, core).
Axes of the slice: x: 2, y: 2, z: 4, core: 2. Of those that a mesh axis runs over, the one named last changes fastest.
Arguments:
- latent: bfloat16 [4, 64, 128, 16], P(None, 'row', 'col')
- conv_weight: bfloat16 [432, 2560], replicated, may hold values from -0.3125 to 0.3125
- conv_bias: float32 [2560], replicated, may hold values from -3 to 3
- norm_gain: float32 [2560], replicated, may hold values from 0.1 to 1.9
- norm_bias: float32 [2560], replicated, may hold values from -3 to 3
- qkv_weight: bfloat16 [2560, 3840], replicated
- shifts: int32 [3], replicated, may hold values from 0 to 7, as said below
Outputs:
- attended: bfloat16 [4, 64, 128, 1280], P(None, 'row', 'col')
The draws below stay inside these ranges and needn't reach their ends.
Inputs may be any that keep to these rules, and one draw needn't show every extreme that they name: shifts[0] is below 2, shifts[1] below 8, shifts[2] below 8.
All inputs are finite; a program needn't handle non-finite values.
Results may differ from the reference program's by a relative error of at most 0.007.
The reference program's roundings to bfloat16 on the way count: a program that leaves them out, or rounds other values in their place, can miss the bound.
Values may be sent and summed in bfloat16 or wider, within the bound.
A program may use at most 192 MiB of HBM per device.

```python
import jax
import jax.numpy as jnp
from jax import lax

CL = 16
GROUPS = 32
D = 2560
HEADS = 10
HD = 128
WT = 2
WH = 8
WW = 8
FR = 4
NH = 64
NW = 128


def draw_latent(key, part):
    rows = jnp.arange(NH, dtype=jnp.float32) / NH
    cols = jnp.arange(NW, dtype=jnp.float32) / NW
    ramp = 1.0 + rows[:, None] + cols[None, :]
    base = jnp.clip(jax.random.normal(key, (FR, NH, NW, CL), jnp.float32), -4.0, 4.0)
    return (base * ramp[None, :, :, None]).astype(jnp.bfloat16)


def draw_qkv_weight(key, part):
    width = 3 * HEADS * HD
    base = jnp.clip(jax.random.normal(key, (D, width), jnp.float32), -4.0, 4.0)
    return (base / D ** 0.5).astype(jnp.bfloat16)


def draw_shifts(key, part):
    first = jax.random.randint(jax.random.fold_in(key, 11), (), 0, WT)
    other = jax.random.randint(jax.random.fold_in(key, 12), (), 0, WH)
    picker = jax.random.randint(jax.random.fold_in(key, 13), (), 0, 2)
    second = jnp.where(picker == 0, WH - 1, other)
    third = jnp.where(picker == 0, other, WW - 1)
    return jnp.stack([first, second, third]).astype(jnp.int32)


def normal_values(key, shape, deviation, most, kind=jnp.bfloat16):
    return jnp.clip(deviation * jax.random.normal(key, shape, jnp.float32), -most, most).astype(kind)


def setup_inputs(seed: int = 0) -> dict:
    key_of = jax.random.split(jax.random.key(seed), 8)
    return {
        "latent": draw_latent(jax.random.fold_in(key_of[7], 71), 0),
        "conv_weight": normal_values(key_of[1], (27 * CL, D), (27 * CL) ** -0.5, 0.3125),
        "conv_bias": normal_values(key_of[2], (D,), 0.5, 3.0, jnp.float32),
        "norm_gain": jnp.clip(1.0 + 0.18 * jax.random.normal(key_of[3], (D,), jnp.float32), 0.1, 1.9),
        "norm_bias": normal_values(key_of[4], (D,), 0.5, 3.0, jnp.float32),
        "qkv_weight": draw_qkv_weight(jax.random.fold_in(key_of[7], 71), 0),
        "shifts": draw_shifts(jax.random.fold_in(key_of[7], 71), 0),
    }


def conv_taps(padded, frames, rows, cols):
    padded = jnp.concatenate([padded[:1], padded[:1], padded], 0)
    taps = [padded[a:a + frames, b:b + rows, c:c + cols] for a in range(3) for b in range(3) for c in range(3)]
    return jnp.concatenate(taps, -1).reshape(frames * rows * cols, -1)

def window_attend(block):
    frames, rows, cols = (block.shape[0], block.shape[1], block.shape[2])
    nt, na, nb = (frames // WT, rows // WH, cols // WW)
    grid = block.reshape(nt, WT, na, WH, nb, WW, 3, HEADS, HD)
    grid = grid.transpose(0, 2, 4, 6, 7, 1, 3, 5, 8).reshape(nt, na, nb, 3, HEADS, WT * WH * WW, HD)
    query = grid[:, :, :, 0].astype(jnp.float32)
    keys = grid[:, :, :, 1].astype(jnp.float32)
    values = grid[:, :, :, 2].astype(jnp.float32)
    scores = jnp.einsum('tabhqd,tabhkd->tabhqk', query, keys) * (1.0 / HD ** 0.5)
    probs = jax.nn.softmax(scores, axis=-1).astype(jnp.bfloat16)
    result = jnp.einsum('tabhqk,tabhkd->tabhqd', probs.astype(jnp.float32), values).astype(jnp.bfloat16)
    result = result.reshape(nt, na, nb, HEADS, WT, WH, WW, HD).transpose(0, 4, 1, 5, 2, 6, 3, 7)
    return result.reshape(frames, rows, cols, HEADS * HD)

def reference(latent, conv_weight, conv_bias, norm_gain, norm_bias, qkv_weight, shifts):
    frames, rows, cols = (latent.shape[0], latent.shape[1], latent.shape[2])
    padded = jnp.pad(latent, ((0, 0), (1, 1), (1, 1), (0, 0)))
    stacked = conv_taps(padded, frames, rows, cols)
    hidden = jnp.dot(stacked, conv_weight, preferred_element_type=jnp.float32) + conv_bias
    grouped = hidden.reshape(-1, GROUPS, D // GROUPS)
    mean = lax.optimization_barrier(jnp.mean(grouped, axis=(0, 2)))
    centred = grouped - mean[None, :, None]
    var = lax.optimization_barrier(jnp.mean(centred * centred, axis=(0, 2)))
    normed = (centred / jnp.sqrt(var + 1e-05)[None, :, None]).reshape(-1, D) * norm_gain + norm_bias
    feat = jax.nn.silu(normed).astype(jnp.bfloat16)
    packed = jnp.dot(feat, qkv_weight, preferred_element_type=jnp.float32).astype(jnp.bfloat16)
    packed = packed.reshape(frames, rows, cols, 3 * HEADS * HD)
    rolled = jnp.roll(packed, -shifts[0], axis=0)
    rolled = jnp.roll(rolled, -shifts[1], axis=1)
    rolled = jnp.roll(rolled, -shifts[2], axis=2)
    blocks = rolled.reshape(frames // WT, WT, rows, cols, 3 * HEADS * HD)
    result = lax.map(window_attend, blocks).reshape(frames, rows, cols, HEADS * HD)
    result = jnp.roll(result, shifts[0], axis=0)
    result = jnp.roll(result, shifts[1], axis=1)
    return jnp.roll(result, shifts[2], axis=2)
```

```python
import jax
import jax.numpy as jnp
from jax import lax
from jax.sharding import PartitionSpec as P

GROUPS = 32
D = 2560
HEADS = 10
HD = 128
WT = 2
WH = 8
WW = 8
HALF = 4


def shifted(x, axis, by):
    length = lax.axis_size(axis)
    return lax.ppermute(x, axis, [(i, (i + by) % length) for i in range(length)])


def with_halo(block, axis, dim):
    size = block.shape[dim]
    low = shifted(lax.slice_in_dim(block, size - HALF, size, axis=dim), axis, 1)
    high = shifted(lax.slice_in_dim(block, 0, HALF + 1, axis=dim), axis, -1)
    return jnp.concatenate([low, block, high], axis=dim)


def signed_shift(shift, window):
    return jnp.where(shift <= HALF, shift, shift - window)


def frame_roll(field, start):
    doubled = jnp.concatenate([field, field], 0)
    return lax.dynamic_slice_in_dim(doubled, start, field.shape[0], 0)


def edge_mask(axis, size, offset):
    total = size * lax.axis_size(axis)
    place = (lax.axis_index(axis) * size + offset + jnp.arange(size) + total) % total
    return place != 0, place != total - 1


def patches(latent, shifts, move_row, move_col):
    frames, rows, cols, chans = latent.shape
    field = with_halo(with_halo(latent, "row", 1), "col", 2)
    zero = jnp.zeros((), jnp.int32)
    field = lax.dynamic_slice(
        field, (zero, move_row + HALF - 1, move_col + HALF - 1, zero), (frames, rows + 2, cols + 2, chans)
    )
    before, after = edge_mask("col", cols, move_col)
    pieces = []
    for c, mask in ((0, before), (1, None), (2, after)):
        piece = field[:, :, c : c + cols]
        if mask is not None:
            piece = jnp.where(mask[None, None, :, None], piece, 0)
        pieces.append(piece)
    field = jnp.concatenate(pieces, -1)
    padded = jnp.concatenate([field[:1], field[:1], field], 0)
    above, below = edge_mask("row", rows, move_row)
    taps = []
    for a in range(3):
        moved = frame_roll(padded[a : a + frames], shifts[0])
        for b, mask in ((0, above), (1, None), (2, below)):
            tap = moved[:, b : b + rows]
            if mask is not None:
                tap = jnp.where(mask[None, :, None, None], tap, 0)
            taps.append(tap)
    stacked = jnp.concatenate(taps, -1)
    depth = stacked.shape[-1]
    stacked = stacked.reshape(frames // WT, WT, rows // WH, WH, cols // WW, WW, depth)
    return stacked.transpose(0, 2, 4, 1, 3, 5, 6).reshape(frames * rows * cols, depth)


def window_attend(packed):
    cells = WT * WH * WW
    grid = packed.reshape(-1, cells, 3, HEADS, HD)
    query, keys, values = grid[:, :, 0], grid[:, :, 1], grid[:, :, 2]
    scores = jnp.einsum("wqhd,wkhd->whqk", query, keys, preferred_element_type=jnp.float32) * (
        1.0 / HD**0.5
    )
    probs = jax.nn.softmax(scores, axis=-1).astype(jnp.bfloat16)
    result = jnp.einsum(
        "whqk,wkhd->wqhd", probs, values, preferred_element_type=jnp.float32
    ).astype(jnp.bfloat16)
    return result.reshape(-1, HEADS * HD)


def send_back(result, axis, dim, move, window):
    size = result.shape[dim]

    def branch(by):
        def run(field):
            if by == 0:
                return field
            if by > 0:
                arrived = shifted(lax.slice_in_dim(field, size - by, size, axis=dim), axis, 1)
                kept = lax.slice_in_dim(field, 0, size - by, axis=dim)
                return jnp.concatenate([arrived, kept], dim)
            arrived = shifted(lax.slice_in_dim(field, 0, -by, axis=dim), axis, -1)
            kept = lax.slice_in_dim(field, -by, size, axis=dim)
            return jnp.concatenate([kept, arrived], dim)

        return run

    least = HALF + 1 - window
    return lax.switch(move - least, [branch(by) for by in range(least, HALF + 1)], result)


def per_device(latent, conv_weight, conv_bias, norm_gain, norm_bias, qkv_weight, shifts):
    frames, rows, cols = (latent.shape[0], latent.shape[1], latent.shape[2])
    move_row = signed_shift(shifts[1], WH)
    move_col = signed_shift(shifts[2], WW)
    stacked = patches(latent, shifts, move_row, move_col)
    hidden = jnp.dot(stacked, conv_weight, preferred_element_type=jnp.float32) + conv_bias
    grouped = hidden.reshape(-1, GROUPS, D // GROUPS)
    count = grouped.shape[0] * grouped.shape[2] * lax.axis_size("row") * lax.axis_size("col")
    totals, squares = lax.psum(
        (jnp.sum(grouped, axis=(0, 2)), jnp.sum(grouped * grouped, axis=(0, 2))), ("row", "col")
    )
    mean = totals / count
    var = squares / count - mean * mean
    centred = grouped - mean[None, :, None]
    normed = (centred / jnp.sqrt(var + 1e-05)[None, :, None]).reshape(-1, D) * norm_gain + norm_bias
    feat = jax.nn.silu(normed).astype(jnp.bfloat16)
    packed = jnp.dot(feat, qkv_weight, preferred_element_type=jnp.float32).astype(jnp.bfloat16)
    result = window_attend(packed)
    result = result.reshape(frames // WT, rows // WH, cols // WW, WT, WH, WW, -1)
    result = result.transpose(0, 3, 1, 4, 2, 5, 6).reshape(frames, rows, cols, -1)
    result = frame_roll(result, frames - shifts[0])
    result = send_back(result, "row", 1, move_row, WH)
    return send_back(result, "col", 2, move_col, WW)


def solution(mesh):
    in_specs = (P(None, "row", "col", None), P(), P(), P(), P(), P(), P())
    out_specs = P(None, "row", "col", None)
    return jax.shard_map(
        per_device, mesh=mesh, in_specs=in_specs, out_specs=out_specs, check_vma=False
    )
```

```python
import functools
import math

import jax
import jax.numpy as jnp
from jax import lax
from jax.experimental import pallas as pl
from jax.experimental.pallas import tpu as pltpu
from jax.sharding import PartitionSpec as P

GROUPS = 32
D = 2560
HEADS = 10
HD = 128
WT = 2
WH = 8
WW = 8
HALF = 4


def shifted(x, axis, by):
    length = lax.axis_size(axis)
    return lax.ppermute(x, axis, [(i, (i + by) % length) for i in range(length)])


def with_halo(block, axis, dim):
    size = block.shape[dim]
    low = shifted(lax.slice_in_dim(block, size - HALF, size, axis=dim), axis, 1)
    high = shifted(lax.slice_in_dim(block, 0, HALF + 1, axis=dim), axis, -1)
    return jnp.concatenate([low, block, high], axis=dim)


def signed_shift(shift, window):
    return jnp.where(shift <= HALF, shift, shift - window)


def frame_roll(field, start):
    doubled = jnp.concatenate([field, field], 0)
    return lax.dynamic_slice_in_dim(doubled, start, field.shape[0], 0)


def edge_mask(axis, size, offset):
    total = size * lax.axis_size(axis)
    place = (lax.axis_index(axis) * size + offset + jnp.arange(size) + total) % total
    return place != 0, place != total - 1


def patches(latent, shifts, move_row, move_col):
    frames, rows, cols, chans = latent.shape
    field = with_halo(with_halo(latent, "row", 1), "col", 2)
    zero = jnp.zeros((), jnp.int32)
    field = lax.dynamic_slice(
        field, (zero, move_row + HALF - 1, move_col + HALF - 1, zero), (frames, rows + 2, cols + 2, chans)
    )
    before, after = edge_mask("col", cols, move_col)
    pieces = []
    for c, mask in ((0, before), (1, None), (2, after)):
        piece = field[:, :, c : c + cols]
        if mask is not None:
            piece = jnp.where(mask[None, None, :, None], piece, 0)
        pieces.append(piece)
    field = jnp.concatenate(pieces, -1)
    padded = jnp.concatenate([field[:1], field[:1], field], 0)
    above, below = edge_mask("row", rows, move_row)
    taps = []
    for a in range(3):
        moved = frame_roll(padded[a : a + frames], shifts[0])
        for b, mask in ((0, above), (1, None), (2, below)):
            tap = moved[:, b : b + rows]
            if mask is not None:
                tap = jnp.where(mask[None, :, None, None], tap, 0)
            taps.append(tap)
    stacked = jnp.concatenate(taps, -1)
    depth = stacked.shape[-1]
    stacked = stacked.reshape(frames // WT, WT, rows // WH, WH, cols // WW, WW, depth)
    return stacked.transpose(0, 2, 4, 1, 3, 5, 6).reshape(frames * rows * cols, depth)


CELLS = WT * WH * WW
PAIR = 2 * HD


def attend_kernel(
    dims, stacked, conv_weight, slope, offset, wq, wk, wv, shifts, out, feat, qkv
):
    frames, rows, cols = dims
    total = frames * rows * cols

    @pl.when(pl.program_id(0) == 0)
    def _():
        part = 256

        @pl.loop(0, total // part)
        def _(i):
            start = pl.multiple_of(i * part, part)
            block = stacked[pl.ds(start, part), :]
            for n in range(0, D, 512):
                hidden = jnp.dot(
                    block, conv_weight[:, n : n + 512], preferred_element_type=jnp.float32
                )
                half = hidden * slope[:, n : n + 512] + offset[:, n : n + 512]
                feat[pl.ds(start, part), n : n + 512] = (half + half * jnp.tanh(half)).astype(
                    jnp.bfloat16
                )

    def project(start):
        lines = pl.ds(start, CHUNK)
        for j, weight in enumerate((wq, wk, wv)):
            qkv[lines, j * PAIR : (j + 1) * PAIR] = jnp.dot(
                feat[lines, :], weight[...], preferred_element_type=jnp.float32
            ).astype(jnp.bfloat16)

    def attend(start, head):
        lines = pl.ds(start, CELLS)
        query = qkv[lines, head * HD : (head + 1) * HD]
        keys = qkv[lines, PAIR + head * HD : PAIR + (head + 1) * HD]
        values = qkv[lines, 2 * PAIR + head * HD : 2 * PAIR + (head + 1) * HD]
        scores = lax.dot_general(
            query, keys, (((1,), (1,)), ((), ())), preferred_element_type=jnp.float32
        )
        most = jnp.max(scores, axis=-1, keepdims=True)
        powers = jnp.exp2((scores - most) * (math.log2(math.e) / HD**0.5))
        probs = powers * (1.0 / jnp.sum(powers, axis=-1, keepdims=True))
        return jnp.dot(probs.astype(jnp.bfloat16), values, preferred_element_type=jnp.float32)

    across = cols // WW

    def attend_rows(group):
        t, a = group // (rows // WH), group % (rows // WH)
        for head in range(2):
            parts = [
                attend((group * across + b) * CELLS, head).reshape(WT, WH, WW, HD) for b in range(across)
            ]
            merged = jnp.concatenate(parts, 2).astype(jnp.bfloat16)
            for dt in range(WT):
                frame = lax.rem(t * WT + dt + shifts[0], frames)
                out[frame, a * WH : (a + 1) * WH, :, head * HD : (head + 1) * HD] = merged[dt]

    groups = CHUNK // (across * CELLS)
    project(0)
    for start in range(0, total, CHUNK):
        if start + CHUNK < total:
            project(start + CHUNK)
        first = start // (across * CELLS)
        for group in range(first, first + groups):
            attend_rows(group)


CHUNK = 512


def attend(dims, stacked, conv_weight, slope, offset, qkv_weight, shifts):
    frames, rows, cols = dims
    total = frames * rows * cols
    steps = HEADS // 2

    def whole(x):
        return pl.BlockSpec(x.shape, lambda h: (0,) * x.ndim, pipeline_mode=pl.Buffered(1))

    def columns(j):
        return pl.BlockSpec((D, PAIR), lambda h: (0, j * steps + h))

    return pl.pallas_call(
        functools.partial(attend_kernel, dims),
        grid=(steps,),
        out_shape=jax.ShapeDtypeStruct((frames, rows, cols, HEADS * HD), jnp.bfloat16),
        in_specs=[
            whole(stacked),
            whole(conv_weight),
            whole(slope),
            whole(offset),
            columns(0),
            columns(1),
            columns(2),
            pl.BlockSpec(memory_space=pltpu.SMEM),
        ],
        out_specs=pl.BlockSpec((frames, rows, cols, PAIR), lambda h: (0, 0, 0, h)),
        scratch_shapes=[
            pltpu.VMEM((total, D), jnp.bfloat16),
            pltpu.VMEM((total, 3 * PAIR), jnp.bfloat16),
        ],
        compiler_params=pltpu.CompilerParams(vmem_limit_bytes=48 * 1024 * 1024),
    )(stacked, conv_weight, slope, offset, qkv_weight, qkv_weight, qkv_weight, shifts)


def send_back(result, axis, dim, move, window):
    size = result.shape[dim]

    def branch(by):
        def run(field):
            if by == 0:
                return field
            if by > 0:
                arrived = shifted(lax.slice_in_dim(field, size - by, size, axis=dim), axis, 1)
                kept = lax.slice_in_dim(field, 0, size - by, axis=dim)
                return jnp.concatenate([arrived, kept], dim)
            arrived = shifted(lax.slice_in_dim(field, 0, -by, axis=dim), axis, -1)
            kept = lax.slice_in_dim(field, -by, size, axis=dim)
            return jnp.concatenate([kept, arrived], dim)

        return run

    least = HALF + 1 - window
    return lax.switch(move - least, [branch(by) for by in range(least, HALF + 1)], result)


def per_device(latent, conv_weight, conv_bias, norm_gain, norm_bias, qkv_weight, shifts):
    frames, rows, cols = (latent.shape[0], latent.shape[1], latent.shape[2])
    move_row = signed_shift(shifts[1], WH)
    move_col = signed_shift(shifts[2], WW)
    stacked = patches(latent, shifts, move_row, move_col)
    hidden = jnp.dot(stacked, conv_weight, preferred_element_type=jnp.float32) + conv_bias
    grouped = hidden.reshape(-1, GROUPS, D // GROUPS)
    count = grouped.shape[0] * grouped.shape[2] * lax.axis_size("row") * lax.axis_size("col")
    totals, squares = lax.psum(
        (jnp.sum(grouped, axis=(0, 2)), jnp.sum(grouped * grouped, axis=(0, 2))), ("row", "col")
    )
    mean = totals / count
    var = squares / count - mean * mean
    scale = lax.rsqrt(var + 1e-05)
    mean, scale = (jnp.repeat(mean, D // GROUPS), jnp.repeat(scale, D // GROUPS))
    slope = 0.5 * scale * norm_gain
    offset = (conv_bias - mean) * slope + 0.5 * norm_bias
    result = attend(
        (frames, rows, cols), stacked, conv_weight, slope[None], offset[None], qkv_weight, shifts
    )
    result = send_back(result, "row", 1, move_row, WH)
    return send_back(result, "col", 2, move_col, WW)


def solution(mesh):
    in_specs = (P(None, "row", "col", None), P(), P(), P(), P(), P(), P())
    out_specs = P(None, "row", "col", None)
    return jax.shard_map(
        per_device, mesh=mesh, in_specs=in_specs, out_specs=out_specs, check_vma=False
    )
```

```python
import functools
import math

import jax
import jax.numpy as jnp
from jax import lax
from jax.experimental import pallas as pl
from jax.experimental.pallas import tpu as pltpu
from jax.sharding import PartitionSpec as P

GROUPS = 32
D = 2560
HEADS = 10
HD = 128
WT = 2
WH = 8
WW = 8
HALF = 4


def shifted(x, axis, by):
    length = lax.axis_size(axis)
    return lax.ppermute(x, axis, [(i, (i + by) % length) for i in range(length)])


def with_halo(block, axis, dim):
    size = block.shape[dim]
    low = shifted(lax.slice_in_dim(block, size - HALF, size, axis=dim), axis, 1)
    high = shifted(lax.slice_in_dim(block, 0, HALF + 1, axis=dim), axis, -1)
    return jnp.concatenate([low, block, high], axis=dim)


def signed_shift(shift, window):
    return jnp.where(shift <= HALF, shift, shift - window)


def frame_roll(field, start):
    doubled = jnp.concatenate([field, field], 0)
    return lax.dynamic_slice_in_dim(doubled, start, field.shape[0], 0)


def edge_mask(axis, size, offset):
    total = size * lax.axis_size(axis)
    place = (lax.axis_index(axis) * size + offset + jnp.arange(size) + total) % total
    return place != 0, place != total - 1


def patches(latent, shifts, move_row, move_col):
    frames, rows, cols, chans = latent.shape
    field = with_halo(with_halo(latent, "row", 1), "col", 2)
    zero = jnp.zeros((), jnp.int32)
    field = lax.dynamic_slice(
        field, (zero, move_row + HALF - 1, move_col + HALF - 1, zero), (frames, rows + 2, cols + 2, chans)
    )
    before, after = edge_mask("col", cols, move_col)
    pieces = []
    for c, mask in ((0, before), (1, None), (2, after)):
        piece = field[:, :, c : c + cols]
        if mask is not None:
            piece = jnp.where(mask[None, None, :, None], piece, 0)
        pieces.append(piece)
    field = jnp.concatenate(pieces, -1)
    padded = jnp.concatenate([field[:1], field[:1], field], 0)
    above, below = edge_mask("row", rows, move_row)
    taps = []
    for a in range(3):
        moved = frame_roll(padded[a : a + frames], shifts[0])
        for b, mask in ((0, above), (1, None), (2, below)):
            tap = moved[:, b : b + rows]
            if mask is not None:
                tap = jnp.where(mask[None, :, None, None], tap, 0)
            taps.append(tap)
    stacked = jnp.concatenate(taps, -1)
    depth = stacked.shape[-1]
    stacked = stacked.reshape(frames // WT, WT, rows // WH, WH, cols // WW, WW, depth)
    return stacked.transpose(0, 2, 4, 1, 3, 5, 6).reshape(frames * rows * cols, depth)


CELLS = WT * WH * WW
PAIR = 2 * HD


def attend_kernel(
    dims, stacked, conv_weight, slope, offset, wq, wk, wv, shifts, out, feat, qkv
):
    frames, rows, cols = dims
    total = frames * rows * cols

    @pl.when(pl.program_id(0) == 0)
    def _():
        part = 256

        @pl.loop(0, total // part)
        def _(i):
            start = pl.multiple_of(i * part, part)
            block = stacked[pl.ds(start, part), :]
            for n in range(0, D, 512):
                hidden = jnp.dot(
                    block, conv_weight[:, n : n + 512], preferred_element_type=jnp.float32
                )
                half = hidden * slope[:, n : n + 512] + offset[:, n : n + 512]
                feat[pl.ds(start, part), n : n + 512] = (half + half * jnp.tanh(half)).astype(
                    jnp.bfloat16
                )

    def project(start):
        lines = pl.ds(start, CHUNK)
        for j, weight in enumerate((wq, wk, wv)):
            qkv[lines, j * PAIR : (j + 1) * PAIR] = jnp.dot(
                feat[lines, :], weight[...], preferred_element_type=jnp.float32
            ).astype(jnp.bfloat16)

    def attend(start, head):
        lines = pl.ds(start, CELLS)
        query = qkv[lines, head * HD : (head + 1) * HD]
        keys = qkv[lines, PAIR + head * HD : PAIR + (head + 1) * HD]
        values = qkv[lines, 2 * PAIR + head * HD : 2 * PAIR + (head + 1) * HD]
        scores = lax.dot_general(
            query, keys, (((1,), (1,)), ((), ())), preferred_element_type=jnp.float32
        )
        most = jnp.max(scores, axis=-1, keepdims=True)
        powers = jnp.exp2((scores - most) * (math.log2(math.e) / HD**0.5))
        probs = powers * (1.0 / jnp.sum(powers, axis=-1, keepdims=True))
        return jnp.dot(probs.astype(jnp.bfloat16), values, preferred_element_type=jnp.float32)

    across = cols // WW

    def attend_rows(group):
        t, a = group // (rows // WH), group % (rows // WH)
        for head in range(2):
            parts = [
                attend((group * across + b) * CELLS, head).reshape(WT, WH, WW, HD) for b in range(across)
            ]
            merged = jnp.concatenate(parts, 2).astype(jnp.bfloat16)
            for dt in range(WT):
                frame = lax.rem(t * WT + dt + shifts[0], frames)
                out[frame, a * WH : (a + 1) * WH, :, head * HD : (head + 1) * HD] = merged[dt]

    groups = CHUNK // (across * CELLS)
    project(0)
    for start in range(0, total, CHUNK):
        if start + CHUNK < total:
            project(start + CHUNK)
        first = start // (across * CELLS)
        for group in range(first, first + groups):
            attend_rows(group)


CHUNK = 512


def attend(dims, stacked, conv_weight, slope, offset, qkv_weight, shifts):
    frames, rows, cols = dims
    total = frames * rows * cols
    steps = HEADS // 2

    def whole(x):
        return pl.BlockSpec(x.shape, lambda h: (0,) * x.ndim, pipeline_mode=pl.Buffered(1))

    def columns(j):
        return pl.BlockSpec((D, PAIR), lambda h: (0, j * steps + h))

    return pl.pallas_call(
        functools.partial(attend_kernel, dims),
        grid=(steps,),
        out_shape=jax.ShapeDtypeStruct((frames, rows, cols, HEADS * HD), jnp.bfloat16),
        in_specs=[
            whole(stacked),
            whole(conv_weight),
            whole(slope),
            whole(offset),
            columns(0),
            columns(1),
            columns(2),
            pl.BlockSpec(memory_space=pltpu.SMEM),
        ],
        out_specs=pl.BlockSpec((frames, rows, cols, PAIR), lambda h: (0, 0, 0, h)),
        scratch_shapes=[
            pltpu.VMEM((total, D), jnp.bfloat16),
            pltpu.VMEM((total, 3 * PAIR), jnp.bfloat16),
        ],
        compiler_params=pltpu.CompilerParams(vmem_limit_bytes=48 * 1024 * 1024),
    )(stacked, conv_weight, slope, offset, qkv_weight, qkv_weight, qkv_weight, shifts)


def sum_kernel(axes, block, out, arrived, part, send_sems, recv_sems):
    peers = []
    for axis in axes:
        count = lax.axis_size(axis)
        me = lax.axis_index(axis)
        peers.append([{axis: lax.rem(me + k, count)} for k in range(1, count)])
    barrier = pltpu.get_barrier_semaphore()
    for peer in peers[0] + peers[1]:
        pl.semaphore_signal(barrier, inc=1, device_id=peer, device_id_type=pl.DeviceIdType.MESH)
    pl.semaphore_wait(barrier, len(peers[0]) + len(peers[1]))
    part[0] = block[...]
    slot = 0
    for phase, group in enumerate(peers):
        copies = []
        for k, peer in enumerate(group):
            copies.append(
                pltpu.make_async_remote_copy(
                    src_ref=part.at[phase],
                    dst_ref=arrived.at[slot + k],
                    send_sem=send_sems.at[slot + k],
                    recv_sem=recv_sems.at[slot + k],
                    device_id=peer,
                    device_id_type=pl.DeviceIdType.MESH,
                )
            )
            copies[-1].start()
        total = part[phase]
        for k, copy in enumerate(copies):
            copy.wait()
            total = total + arrived[slot + k]
        part[phase + 1] = total
        slot += len(group)
    out[...] = part[2]


def sum_over(block, axes):
    count = sum(lax.axis_size(axis) - 1 for axis in axes)
    return pl.pallas_call(
        functools.partial(sum_kernel, axes),
        out_shape=jax.ShapeDtypeStruct(block.shape, jnp.float32),
        in_specs=[pl.BlockSpec(memory_space=pltpu.VMEM)],
        out_specs=pl.BlockSpec(memory_space=pltpu.VMEM),
        scratch_shapes=[
            pltpu.VMEM((count,) + block.shape, jnp.float32),
            pltpu.VMEM((3,) + block.shape, jnp.float32),
            pltpu.SemaphoreType.DMA((count,)),
            pltpu.SemaphoreType.DMA((count,)),
        ],
        compiler_params=pltpu.CompilerParams(collective_id=1, has_side_effects=True),
    )(block)


def send_back(result, axis, dim, move, window):
    size = result.shape[dim]

    def branch(by):
        def run(field):
            if by == 0:
                return field
            if by > 0:
                arrived = shifted(lax.slice_in_dim(field, size - by, size, axis=dim), axis, 1)
                kept = lax.slice_in_dim(field, 0, size - by, axis=dim)
                return jnp.concatenate([arrived, kept], dim)
            arrived = shifted(lax.slice_in_dim(field, 0, -by, axis=dim), axis, -1)
            kept = lax.slice_in_dim(field, -by, size, axis=dim)
            return jnp.concatenate([kept, arrived], dim)

        return run

    least = HALF + 1 - window
    return lax.switch(move - least, [branch(by) for by in range(least, HALF + 1)], result)


def per_device(latent, conv_weight, conv_bias, norm_gain, norm_bias, qkv_weight, shifts):
    frames, rows, cols = (latent.shape[0], latent.shape[1], latent.shape[2])
    move_row = signed_shift(shifts[1], WH)
    move_col = signed_shift(shifts[2], WW)
    stacked = patches(latent, shifts, move_row, move_col)
    hidden = jnp.dot(stacked, conv_weight, preferred_element_type=jnp.float32) + conv_bias
    grouped = hidden.reshape(-1, GROUPS, D // GROUPS)
    count = grouped.shape[0] * grouped.shape[2] * lax.axis_size("row") * lax.axis_size("col")
    sums = jnp.stack([jnp.sum(grouped, axis=(0, 2)), jnp.sum(grouped * grouped, axis=(0, 2))])
    sums = sum_over(jnp.pad(sums, ((0, 6), (0, 128 - GROUPS))), ("col", "row"))
    totals, squares = sums[0, :GROUPS], sums[1, :GROUPS]
    mean = totals / count
    var = squares / count - mean * mean
    scale = lax.rsqrt(var + 1e-05)
    mean, scale = (jnp.repeat(mean, D // GROUPS), jnp.repeat(scale, D // GROUPS))
    slope = 0.5 * scale * norm_gain
    offset = (conv_bias - mean) * slope + 0.5 * norm_bias
    result = attend(
        (frames, rows, cols), stacked, conv_weight, slope[None], offset[None], qkv_weight, shifts
    )
    result = send_back(result, "row", 1, move_row, WH)
    return send_back(result, "col", 2, move_col, WW)


def solution(mesh):
    in_specs = (P(None, "row", "col", None), P(), P(), P(), P(), P(), P())
    out_specs = P(None, "row", "col", None)
    return jax.shard_map(
        per_device, mesh=mesh, in_specs=in_specs, out_specs=out_specs, check_vma=False
    )
```

```python
import functools
import math

import jax
import jax.numpy as jnp
from jax import lax
from jax.experimental import pallas as pl
from jax.experimental.pallas import tpu as pltpu
from jax.sharding import PartitionSpec as P

GROUPS = 32
D = 2560
HEADS = 10
HD = 128
WT = 2
WH = 8
WW = 8
HALF = 4


def shifted(x, axis, by):
    length = lax.axis_size(axis)
    return lax.ppermute(x, axis, [(i, (i + by) % length) for i in range(length)])


def with_halo(block, axis, dim):
    size = block.shape[dim]
    low = shifted(lax.slice_in_dim(block, size - HALF, size, axis=dim), axis, 1)
    high = shifted(lax.slice_in_dim(block, 0, HALF + 1, axis=dim), axis, -1)
    return jnp.concatenate([low, block, high], axis=dim)


def signed_shift(shift, window):
    return jnp.where(shift <= HALF, shift, shift - window)


def frame_roll(field, start):
    doubled = jnp.concatenate([field, field], 0)
    return lax.dynamic_slice_in_dim(doubled, start, field.shape[0], 0)


def edge_mask(axis, size, offset):
    total = size * lax.axis_size(axis)
    place = (lax.axis_index(axis) * size + offset + jnp.arange(size) + total) % total
    return place != 0, place != total - 1


def patches(latent, shifts, move_row, move_col):
    frames, rows, cols, chans = latent.shape
    field = with_halo(with_halo(latent, "row", 1), "col", 2)
    zero = jnp.zeros((), jnp.int32)
    field = lax.dynamic_slice(
        field, (zero, move_row + HALF - 1, move_col + HALF - 1, zero), (frames, rows + 2, cols + 2, chans)
    )
    before, after = edge_mask("col", cols, move_col)
    pieces = []
    for c, mask in ((0, before), (1, None), (2, after)):
        piece = field[:, :, c : c + cols]
        if mask is not None:
            piece = jnp.where(mask[None, None, :, None], piece, 0)
        pieces.append(piece)
    field = jnp.concatenate(pieces, -1)
    padded = jnp.concatenate([field[:1], field[:1], field], 0)
    above, below = edge_mask("row", rows, move_row)
    taps = []
    for a in range(3):
        moved = frame_roll(padded[a : a + frames], shifts[0])
        for b, mask in ((0, above), (1, None), (2, below)):
            tap = moved[:, b : b + rows]
            if mask is not None:
                tap = jnp.where(mask[None, :, None, None], tap, 0)
            taps.append(tap)
    stacked = jnp.concatenate(taps, -1)
    depth = stacked.shape[-1]
    stacked = stacked.reshape(frames // WT, WT, rows // WH, WH, cols // WW, WW, depth)
    return stacked.transpose(0, 2, 4, 1, 3, 5, 6).reshape(frames * rows * cols, depth)


CELLS = WT * WH * WW
PAIR = 2 * HD


def attend_kernel(
    dims, stacked, conv_weight, slope, offset, wq, wk, wv, shifts, out, feat, qkv
):
    frames, rows, cols = dims
    total = frames * rows * cols

    @pl.when(pl.program_id(0) == 0)
    def _():
        part = 256

        @pl.loop(0, total // part)
        def _(i):
            start = pl.multiple_of(i * part, part)
            block = stacked[pl.ds(start, part), :]
            for n in range(0, D, 512):
                hidden = jnp.dot(
                    block, conv_weight[:, n : n + 512], preferred_element_type=jnp.float32
                )
                half = hidden * slope[:, n : n + 512] + offset[:, n : n + 512]
                feat[pl.ds(start, part), n : n + 512] = (half + half * jnp.tanh(half)).astype(
                    jnp.bfloat16
                )

    def project(start, j):
        if start < total:
            lines = slice(start, start + CHUNK)
            qkv[lines, j * PAIR : (j + 1) * PAIR] = jnp.dot(
                feat[lines, :], (wq, wk, wv)[j][...], preferred_element_type=jnp.float32
            ).astype(jnp.bfloat16)

    def part(item, j):
        window, head = item
        first = j * PAIR + head * HD
        return qkv[window * CELLS : (window + 1) * CELLS, first : first + HD]

    def score(item):
        return lax.dot_general(
            part(item, 0), part(item, 1), (((1,), (1,)), ((), ())), preferred_element_type=jnp.float32
        )

    def softmax(scores):
        most = [jnp.max(x, axis=-1, keepdims=True) for x in scores]
        powers = [
            jnp.exp2((x - m) * (math.log2(math.e) / HD**0.5)) for x, m in zip(scores, most)
        ]
        sums = [jnp.sum(x, axis=-1, keepdims=True) for x in powers]
        return [(x * (1.0 / t)).astype(jnp.bfloat16) for x, t in zip(powers, sums)]

    across = cols // WW

    def store(group, head, results):
        t, a = group // (rows // WH), group % (rows // WH)
        merged = jnp.concatenate([x.reshape(WT, WH, WW, HD) for x in results], 2).astype(jnp.bfloat16)
        for dt in range(WT):
            frame = lax.rem(t * WT + dt + shifts[0], frames)
            out[frame, a * WH : (a + 1) * WH, :, head * HD : (head + 1) * HD] = merged[dt]

    for j in range(3):
        project(0, j)
    for start in range(0, total, CHUNK):
        first = start // CELLS
        items = [(w, head) for head in range(2) for w in range(first, first + CHUNK // CELLS)]
        scores = [score(item) for item in items]
        project(start + CHUNK, 0)
        probs = softmax(scores)
        project(start + CHUNK, 1)
        results = {
            item: jnp.dot(p, part(item, 2), preferred_element_type=jnp.float32)
            for item, p in zip(items, probs)
        }
        project(start + CHUNK, 2)
        for head in range(2):
            for w in range(first, first + CHUNK // CELLS, across):
                store(w // across, head, [results[w + b, head] for b in range(across)])


CHUNK = 512


def attend(dims, stacked, conv_weight, slope, offset, qkv_weight, shifts):
    frames, rows, cols = dims
    total = frames * rows * cols
    steps = HEADS // 2

    def whole(x):
        return pl.BlockSpec(x.shape, lambda h: (0,) * x.ndim, pipeline_mode=pl.Buffered(1))

    def columns(j):
        return pl.BlockSpec((D, PAIR), lambda h: (0, j * steps + h))

    return pl.pallas_call(
        functools.partial(attend_kernel, dims),
        grid=(steps,),
        out_shape=jax.ShapeDtypeStruct((frames, rows, cols, HEADS * HD), jnp.bfloat16),
        in_specs=[
            whole(stacked),
            whole(conv_weight),
            whole(slope),
            whole(offset),
            columns(0),
            columns(1),
            columns(2),
            pl.BlockSpec(memory_space=pltpu.SMEM),
        ],
        out_specs=pl.BlockSpec((frames, rows, cols, PAIR), lambda h: (0, 0, 0, h)),
        scratch_shapes=[
            pltpu.VMEM((total, D), jnp.bfloat16),
            pltpu.VMEM((total, 3 * PAIR), jnp.bfloat16),
        ],
        compiler_params=pltpu.CompilerParams(vmem_limit_bytes=48 * 1024 * 1024),
    )(stacked, conv_weight, slope, offset, qkv_weight, qkv_weight, qkv_weight, shifts)


def sum_kernel(axes, block, out, arrived, part, send_sems, recv_sems):
    peers = []
    for axis in axes:
        count = lax.axis_size(axis)
        me = lax.axis_index(axis)
        peers.append([{axis: lax.rem(me + k, count)} for k in range(1, count)])
    barrier = pltpu.get_barrier_semaphore()
    for peer in peers[0] + peers[1]:
        pl.semaphore_signal(barrier, inc=1, device_id=peer, device_id_type=pl.DeviceIdType.MESH)
    pl.semaphore_wait(barrier, len(peers[0]) + len(peers[1]))
    part[0] = block[...]
    slot = 0
    for phase, group in enumerate(peers):
        copies = []
        for k, peer in enumerate(group):
            copies.append(
                pltpu.make_async_remote_copy(
                    src_ref=part.at[phase],
                    dst_ref=arrived.at[slot + k],
                    send_sem=send_sems.at[slot + k],
                    recv_sem=recv_sems.at[slot + k],
                    device_id=peer,
                    device_id_type=pl.DeviceIdType.MESH,
                )
            )
            copies[-1].start()
        total = part[phase]
        for k, copy in enumerate(copies):
            copy.wait()
            total = total + arrived[slot + k]
        part[phase + 1] = total
        slot += len(group)
    out[...] = part[2]


def sum_over(block, axes):
    count = sum(lax.axis_size(axis) - 1 for axis in axes)
    return pl.pallas_call(
        functools.partial(sum_kernel, axes),
        out_shape=jax.ShapeDtypeStruct(block.shape, jnp.float32),
        in_specs=[pl.BlockSpec(memory_space=pltpu.VMEM)],
        out_specs=pl.BlockSpec(memory_space=pltpu.VMEM),
        scratch_shapes=[
            pltpu.VMEM((count,) + block.shape, jnp.float32),
            pltpu.VMEM((3,) + block.shape, jnp.float32),
            pltpu.SemaphoreType.DMA((count,)),
            pltpu.SemaphoreType.DMA((count,)),
        ],
        compiler_params=pltpu.CompilerParams(collective_id=1, has_side_effects=True),
    )(block)


def send_back(result, axis, dim, move, window):
    size = result.shape[dim]

    def branch(by):
        def run(field):
            if by == 0:
                return field
            if by > 0:
                arrived = shifted(lax.slice_in_dim(field, size - by, size, axis=dim), axis, 1)
                kept = lax.slice_in_dim(field, 0, size - by, axis=dim)
                return jnp.concatenate([arrived, kept], dim)
            arrived = shifted(lax.slice_in_dim(field, 0, -by, axis=dim), axis, -1)
            kept = lax.slice_in_dim(field, -by, size, axis=dim)
            return jnp.concatenate([kept, arrived], dim)

        return run

    least = HALF + 1 - window
    return lax.switch(move - least, [branch(by) for by in range(least, HALF + 1)], result)


def per_device(latent, conv_weight, conv_bias, norm_gain, norm_bias, qkv_weight, shifts):
    frames, rows, cols = (latent.shape[0], latent.shape[1], latent.shape[2])
    move_row = signed_shift(shifts[1], WH)
    move_col = signed_shift(shifts[2], WW)
    stacked = patches(latent, shifts, move_row, move_col)
    hidden = jnp.dot(stacked, conv_weight, preferred_element_type=jnp.float32) + conv_bias
    grouped = hidden.reshape(-1, GROUPS, D // GROUPS)
    count = grouped.shape[0] * grouped.shape[2] * lax.axis_size("row") * lax.axis_size("col")
    sums = jnp.stack([jnp.sum(grouped, axis=(0, 2)), jnp.sum(grouped * grouped, axis=(0, 2))])
    sums = sum_over(jnp.pad(sums, ((0, 6), (0, 128 - GROUPS))), ("col", "row"))
    totals, squares = sums[0, :GROUPS], sums[1, :GROUPS]
    mean = totals / count
    var = squares / count - mean * mean
    scale = lax.rsqrt(var + 1e-05)
    mean, scale = (jnp.repeat(mean, D // GROUPS), jnp.repeat(scale, D // GROUPS))
    slope = 0.5 * scale * norm_gain
    offset = (conv_bias - mean) * slope + 0.5 * norm_bias
    result = attend(
        (frames, rows, cols), stacked, conv_weight, slope[None], offset[None], qkv_weight, shifts
    )
    result = send_back(result, "row", 1, move_row, WH)
    return send_back(result, "col", 2, move_col, WW)


def solution(mesh):
    in_specs = (P(None, "row", "col", None), P(), P(), P(), P(), P(), P())
    out_specs = P(None, "row", "col", None)
    return jax.shard_map(
        per_device, mesh=mesh, in_specs=in_specs, out_specs=out_specs, check_vma=False
    )
```

```python
import functools
import math

import jax
import jax.numpy as jnp
from jax import lax
from jax.experimental import pallas as pl
from jax.experimental.pallas import tpu as pltpu
from jax.sharding import PartitionSpec as P

GROUPS = 32
D = 2560
HEADS = 10
HD = 128
WT = 2
WH = 8
WW = 8
HALF = 4


def shifted(x, axis, by):
    length = lax.axis_size(axis)
    return lax.ppermute(x, axis, [(i, (i + by) % length) for i in range(length)])


def with_halo(block, axis, dim):
    size = block.shape[dim]
    low = shifted(lax.slice_in_dim(block, size - HALF, size, axis=dim), axis, 1)
    high = shifted(lax.slice_in_dim(block, 0, HALF + 1, axis=dim), axis, -1)
    return jnp.concatenate([low, block, high], axis=dim)


def signed_shift(shift, window):
    return jnp.where(shift <= HALF, shift, shift - window)


def frame_roll(field, start):
    doubled = jnp.concatenate([field, field], 0)
    return lax.dynamic_slice_in_dim(doubled, start, field.shape[0], 0)


def edge_mask(axis, size, offset):
    total = size * lax.axis_size(axis)
    place = (lax.axis_index(axis) * size + offset + jnp.arange(size) + total) % total
    return place != 0, place != total - 1


def patches(latent, shifts, move_row, move_col):
    frames, rows, cols, chans = latent.shape
    field = with_halo(with_halo(latent, "row", 1), "col", 2)
    zero = jnp.zeros((), jnp.int32)
    field = lax.dynamic_slice(
        field, (zero, move_row + HALF - 1, move_col + HALF - 1, zero), (frames, rows + 2, cols + 2, chans)
    )
    before, after = edge_mask("col", cols, move_col)
    pieces = []
    for c, mask in ((0, before), (1, None), (2, after)):
        piece = field[:, :, c : c + cols]
        if mask is not None:
            piece = jnp.where(mask[None, None, :, None], piece, 0)
        pieces.append(piece)
    field = jnp.concatenate(pieces, -1)
    padded = jnp.concatenate([field[:1], field[:1], field], 0)
    above, below = edge_mask("row", rows, move_row)
    taps = []
    for a in range(3):
        moved = frame_roll(padded[a : a + frames], shifts[0])
        for b, mask in ((0, above), (1, None), (2, below)):
            tap = moved[:, b : b + rows]
            if mask is not None:
                tap = jnp.where(mask[None, :, None, None], tap, 0)
            taps.append(tap)
    stacked = jnp.concatenate(taps, -1)
    depth = stacked.shape[-1]
    stacked = stacked.reshape(frames // WT, WT, rows // WH, WH, cols // WW, WW, depth)
    return stacked.transpose(0, 2, 4, 1, 3, 5, 6).reshape(frames * rows * cols, depth)


CELLS = WT * WH * WW
PAIR = 2 * HD


def attend_kernel(
    dims, stacked, conv_weight, slope, offset, wq, wk, wv, moves, out, feat, qkv
):
    frames, rows, cols = dims
    total = frames * rows * cols

    @pl.when(pl.program_id(0) == 0)
    def _():
        part = 256

        @pl.loop(0, total // part)
        def _(i):
            start = pl.multiple_of(i * part, part)
            block = stacked[pl.ds(start, part), :]
            for n in range(0, D, 512):
                hidden = jnp.dot(
                    block, conv_weight[:, n : n + 512], preferred_element_type=jnp.float32
                )
                half = hidden * slope[:, n : n + 512] + offset[:, n : n + 512]
                feat[pl.ds(start, part), n : n + 512] = (half + half * jnp.tanh(half)).astype(
                    jnp.bfloat16
                )

    def project(start, j):
        if start < total:
            lines = slice(start, start + CHUNK)
            qkv[lines, j * PAIR : (j + 1) * PAIR] = jnp.dot(
                feat[lines, :], (wq, wk, wv)[j][...], preferred_element_type=jnp.float32
            ).astype(jnp.bfloat16)

    def part(item, j):
        window, head = item
        first = j * PAIR + head * HD
        return qkv[window * CELLS : (window + 1) * CELLS, first : first + HD]

    def score(item):
        return lax.dot_general(
            part(item, 0), part(item, 1), (((1,), (1,)), ((), ())), preferred_element_type=jnp.float32
        )

    def softmax(scores):
        most = [jnp.max(x, axis=-1, keepdims=True) for x in scores]
        powers = [
            jnp.exp2((x - m) * (math.log2(math.e) / HD**0.5)) for x, m in zip(scores, most)
        ]
        sums = [jnp.sum(x, axis=-1, keepdims=True) for x in powers]
        return [(x * (1.0 / t)).astype(jnp.bfloat16) for x, t in zip(powers, sums)]

    across = cols // WW

    def store(group, head, results):
        t, a = group // (rows // WH), group % (rows // WH)
        merged = jnp.concatenate([x.reshape(WT, WH, WW, HD) for x in results], 2)
        for dt in range(WT):
            frame = lax.rem(t * WT + dt + moves[0], frames)
            for y in range(WH):
                row = lax.rem(a * WH + y + moves[1], rows)
                line = pltpu.roll(merged[dt, y], moves[2], 0).astype(jnp.bfloat16)
                out[frame, row, :, head * HD : (head + 1) * HD] = line

    for j in range(3):
        project(0, j)
    for start in range(0, total, CHUNK):
        first = start // CELLS
        items = [(w, head) for head in range(2) for w in range(first, first + CHUNK // CELLS)]
        scores = [score(item) for item in items]
        project(start + CHUNK, 0)
        probs = softmax(scores)
        project(start + CHUNK, 1)
        results = {
            item: jnp.dot(p, part(item, 2), preferred_element_type=jnp.float32)
            for item, p in zip(items, probs)
        }
        project(start + CHUNK, 2)
        for head in range(2):
            for w in range(first, first + CHUNK // CELLS, across):
                store(w // across, head, [results[w + b, head] for b in range(across)])


CHUNK = 512


def attend(dims, stacked, conv_weight, slope, offset, qkv_weight, moves):
    frames, rows, cols = dims
    total = frames * rows * cols
    steps = HEADS // 2

    def whole(x):
        return pl.BlockSpec(x.shape, lambda h: (0,) * x.ndim, pipeline_mode=pl.Buffered(1))

    def columns(j):
        return pl.BlockSpec((D, PAIR), lambda h: (0, j * steps + h))

    return pl.pallas_call(
        functools.partial(attend_kernel, dims),
        grid=(steps,),
        out_shape=jax.ShapeDtypeStruct((frames, rows, cols, HEADS * HD), jnp.bfloat16),
        in_specs=[
            whole(stacked),
            whole(conv_weight),
            whole(slope),
            whole(offset),
            columns(0),
            columns(1),
            columns(2),
            pl.BlockSpec(memory_space=pltpu.SMEM),
        ],
        out_specs=pl.BlockSpec((frames, rows, cols, PAIR), lambda h: (0, 0, 0, h)),
        scratch_shapes=[
            pltpu.VMEM((total, D), jnp.bfloat16),
            pltpu.VMEM((total, 3 * PAIR), jnp.bfloat16),
        ],
        compiler_params=pltpu.CompilerParams(vmem_limit_bytes=48 * 1024 * 1024),
    )(stacked, conv_weight, slope, offset, qkv_weight, qkv_weight, qkv_weight, moves)


def sum_kernel(axes, block, out, arrived, part, send_sems, recv_sems):
    peers = []
    for axis in axes:
        count = lax.axis_size(axis)
        me = lax.axis_index(axis)
        peers.append([{axis: lax.rem(me + k, count)} for k in range(1, count)])
    barrier = pltpu.get_barrier_semaphore()
    for peer in peers[0] + peers[1]:
        pl.semaphore_signal(barrier, inc=1, device_id=peer, device_id_type=pl.DeviceIdType.MESH)
    pl.semaphore_wait(barrier, len(peers[0]) + len(peers[1]))
    part[0] = block[...]
    slot = 0
    for phase, group in enumerate(peers):
        copies = []
        for k, peer in enumerate(group):
            copies.append(
                pltpu.make_async_remote_copy(
                    src_ref=part.at[phase],
                    dst_ref=arrived.at[slot + k],
                    send_sem=send_sems.at[slot + k],
                    recv_sem=recv_sems.at[slot + k],
                    device_id=peer,
                    device_id_type=pl.DeviceIdType.MESH,
                )
            )
            copies[-1].start()
        total = part[phase]
        for k, copy in enumerate(copies):
            copy.wait()
            total = total + arrived[slot + k]
        part[phase + 1] = total
        slot += len(group)
    out[...] = part[2]


def sum_over(block, axes):
    count = sum(lax.axis_size(axis) - 1 for axis in axes)
    return pl.pallas_call(
        functools.partial(sum_kernel, axes),
        out_shape=jax.ShapeDtypeStruct(block.shape, jnp.float32),
        in_specs=[pl.BlockSpec(memory_space=pltpu.VMEM)],
        out_specs=pl.BlockSpec(memory_space=pltpu.VMEM),
        scratch_shapes=[
            pltpu.VMEM((count,) + block.shape, jnp.float32),
            pltpu.VMEM((3,) + block.shape, jnp.float32),
            pltpu.SemaphoreType.DMA((count,)),
            pltpu.SemaphoreType.DMA((count,)),
        ],
        compiler_params=pltpu.CompilerParams(collective_id=1, has_side_effects=True),
    )(block)


def send_back(result, axis, dim, move, window, least_sent):
    size = result.shape[dim]

    def branch(by):
        def run(field):
            if by == 0:
                return field
            count = abs(by)
            wide = max(count, least_sent)
            start = 0 if by > 0 else size - wide
            part = lax.slice_in_dim(field, start, start + wide, axis=dim)
            shape = part.shape
            part = lax.optimization_barrier(part.reshape(-1, shape[-1]))
            arrived = lax.optimization_barrier(shifted(part, axis, 1 if by > 0 else -1))
            skip = 0 if by > 0 else wide - count
            arrived = lax.slice_in_dim(arrived.reshape(shape), skip, skip + count, axis=dim)
            return lax.dynamic_update_slice_in_dim(field, arrived, start + skip, dim)

        return run

    least = HALF + 1 - window
    return lax.switch(move - least, [branch(by) for by in range(least, HALF + 1)], result)


def per_device(latent, conv_weight, conv_bias, norm_gain, norm_bias, qkv_weight, shifts):
    frames, rows, cols = (latent.shape[0], latent.shape[1], latent.shape[2])
    move_row = signed_shift(shifts[1], WH)
    move_col = signed_shift(shifts[2], WW)
    stacked = patches(latent, shifts, move_row, move_col)
    hidden = jnp.dot(stacked, conv_weight, preferred_element_type=jnp.float32) + conv_bias
    grouped = hidden.reshape(-1, GROUPS, D // GROUPS)
    count = grouped.shape[0] * grouped.shape[2] * lax.axis_size("row") * lax.axis_size("col")
    sums = jnp.stack([jnp.sum(grouped, axis=(0, 2)), jnp.sum(grouped * grouped, axis=(0, 2))])
    sums = sum_over(jnp.pad(sums, ((0, 6), (0, 128 - GROUPS))), ("col", "row"))
    totals, squares = sums[0, :GROUPS], sums[1, :GROUPS]
    mean = totals / count
    var = squares / count - mean * mean
    scale = lax.rsqrt(var + 1e-05)
    mean, scale = (jnp.repeat(mean, D // GROUPS), jnp.repeat(scale, D // GROUPS))
    slope = 0.5 * scale * norm_gain
    offset = (conv_bias - mean) * slope + 0.5 * norm_bias
    moves = jnp.stack([shifts[0], (move_row + rows) % rows, (move_col + cols) % cols])
    result = attend(
        (frames, rows, cols), stacked, conv_weight, slope[None], offset[None], qkv_weight, moves
    )
    result = send_back(result, "row", 1, move_row, WH, 1)
    return send_back(result, "col", 2, move_col, WW, 2)


def solution(mesh):
    in_specs = (P(None, "row", "col", None), P(), P(), P(), P(), P(), P())
    out_specs = P(None, "row", "col", None)
    return jax.shard_map(
        per_device, mesh=mesh, in_specs=in_specs, out_specs=out_specs, check_vma=False
    )
```
